32 devices in a mesh: grp: 4 (over x, core), gx: 2 (over y), gy: 4 (over z).
Axes of the slice: x: 2, y: 2, z: 4, core: 2. Of those that a mesh axis runs over, the one named last changes fastest.
Arguments:
- pressure_start: float32 [16, 32, 512], P('gx', 'gy', 'grp'), may hold values from -6 to 6
- saturation: float32 [16, 32, 512], P('gx', 'gy', 'grp'), may hold values from 0.1 to 0.9
- permeability: float32 [16, 32, 512], P('gx', 'gy', 'grp'), may hold values from 0.1 to 10
- rock_type: int32 [16, 32, 512], P('gx', 'gy', 'grp'), may hold values from 0 to 3
- rock_table: float32 [5, 4], replicated, may hold values from 0.5 to 3
- well_cells: int32 [64], replicated, may hold values from 0 to 262143
- well_rates: float32 [64], replicated, may hold values from -12 to 12
- owner_map: int32 [2, 4, 4, 64, 1], P('gx', 'gy', 'grp'), may hold values from 0 to 1; in each aligned block of 64 rows (0 to 63, 64 to 127, ..., all dimensions but the last counted through in order) at most 64 rows name the same one
- stiffness: bfloat16 [2, 4, 4, 2, 64, 24, 24], P('gx', 'gy', 'grp'), may hold values from -0.008 to 0.2, as said below
- anchored: int32 [16, 32, 512], P('gx', 'gy', 'grp'), may hold values 0 or 1
Outputs:
- pressure: float32 [16, 32, 512], P('gx', 'gy', 'grp')
- vol_strain: float32 [16, 32, 512], P('gx', 'gy', 'grp')
The draws below stay inside these ranges and needn't reach their ends.
Inputs may be any that keep to these rules, and one draw needn't show every extreme that they name: `owner_map`: of the 64 bricks of one device, at most 64 have the same owner. `stiffness`: the diagonal entries of every block lie between 0.1 and 0.2.
All inputs are finite; a program needn't handle non-finite values. No bound on the sum of `anchored` on one device may be relied on, other than what follows from the above.
Results may differ from the reference program's by a relative error of at most 0.0013.
Values may be sent and summed in bfloat16 or wider, within the bound.
A program may use at most 64 MiB of HBM per device.

```python
import math
import jax
import jax.numpy as jnp
import numpy as np
from jax import lax

CX = 8
CY = 8
CZ = 128
ITERS = 2
FLOW_PASSES = 4
MECH_PASSES = 3
ROCKS = 4
WELLS = 64
SLABS_X = 2
SLABS_Y = 4
LAYERS_Z = 4
BRICKS = 64
CAP = 64
NX = 16
NY = 32
NZ = 512
N_GRP = 4
N_GX = 2
N_GY = 4


def draw_stiffness(key, part):
    block_shape = (SLABS_X, SLABS_Y, LAYERS_Z, SLABS_X, CAP)
    first_key, second_key = jax.random.split(jax.random.fold_in(key, 7))
    diag_part = jax.random.uniform(first_key, block_shape, jnp.float32, 0.101, 0.195)
    off_part = jax.random.uniform(second_key, block_shape + (24, 24), jnp.float32, -0.0079, 0.0079)
    identity = jnp.eye(24, dtype=jnp.float32)
    blocks = off_part * (1.0 - identity) + diag_part[..., None, None] * identity
    return blocks.astype(jnp.bfloat16)


def set_ends(values, key, least, top_value):
    index_at = [jax.random.randint(jax.random.fold_in(key, axis), (), 0, length) for axis, length in enumerate(values.shape)]
    longest = values.shape.index(max(values.shape))
    neighbour = index_at[:longest] + [(index_at[longest] + 1) % values.shape[longest]] + index_at[longest + 1:]
    return values.at[tuple(index_at)].set(least).at[tuple(neighbour)].set(top_value)


def levels(key, dims, shards, least, largest):
    level = 1.0
    for axis_at, shards_of in shards:
        draws = jax.random.uniform(jax.random.fold_in(jax.random.fold_in(key, 6), axis_at), (shards_of,), jnp.float32, least / len(shards), largest / len(shards))
        level = level * jnp.repeat(jnp.exp(draws), dims[axis_at] // shards_of).reshape((-1,) + (1,) * (len(dims) - 1 - axis_at))
    return level


def assign_block(stream_key, own, number, rows, amount, top, most, lean):
    order = jax.random.permutation(stream_key, amount)
    crowded, usual = portions_of(amount, rows * top, most, lean, True), portions_of(amount, rows * top, most, lean, False)
    places = jnp.arange(amount)

    def named(lengths, turn):
        used = int((lengths > 0).sum())
        fixed = max(1, used // 4)
        shifted = fixed + (places - fixed + turn * (used - fixed)) % max(1, amount - fixed)
        return jnp.zeros((amount,), jnp.int32).at[order[jnp.where(places < fixed, places, shifted)]].set(jnp.asarray(lengths, jnp.int32))

    lengths = jnp.where(number % 4 == 0, named(crowded, number // 4), named(usual, number - number // 4 - 1))
    mixed = jax.random.permutation(jax.random.fold_in(own, 3), amount)
    source_of, receiver = mixed[0:amount // 2 * 2:2], mixed[1:amount // 2 * 2:2]
    slack = jnp.minimum(lengths[source_of] - 1, most - lengths[receiver]) // 2
    slack = jnp.where((source_of == order[0]) | (receiver == order[0]) | (lengths[receiver] == 0), 0, jnp.maximum(slack, 0))
    shifted = jax.random.randint(jax.random.fold_in(own, 4), (amount // 2,), 0, 1 << 20) % (slack + 1)
    lengths = lengths.at[source_of].add(-shifted).at[receiver].add(shifted)
    labels = jnp.searchsorted(jnp.cumsum(lengths), jnp.arange(rows * top), side="right").astype(jnp.int32)
    table = labels.reshape(top, rows).T
    table = table[jax.random.permutation(jax.random.fold_in(own, 1), rows)]
    turn = jax.random.randint(jax.random.fold_in(own, 2), (rows, 1), 0, top)
    return jnp.take_along_axis(table, (jnp.arange(top)[None, :] + turn) % top, axis=1)


def portions_of(count, total, limit, skew, full):
    weights = [(1 << 20) // math.isqrt(rank ** skew) + 1 for rank in range(1, count + 1)]
    largest = limit if full else min(limit, max(-(-total // count), total * weights[0] // sum(weights)))
    least = 1 if total - largest >= count - 1 else 0
    holding, spare = [largest] + [least] * (count - 1), total - largest - least * (count - 1)
    while spare > 0:
        candidates = [i for i in range(1, count) if holding[i] < largest] or [i for i in range(1, count) if holding[i] < limit]
        mass, left = sum([weights[i] for i in candidates]), spare
        for i in candidates:
            extra = min(limit - holding[i], max(1, left * weights[i] // mass), spare)
            holding[i] = holding[i] + extra
            spare = spare - extra
    return np.array(holding)


def noise(stream_key, dims, width, reach, shards=(), held_as=jnp.bfloat16):
    loudness = levels(stream_key, dims, shards, -0.22, 0.18) if shards else 1.0
    array = jax.random.normal(stream_key, dims, jnp.float32) * width * loudness
    return jnp.minimum(jnp.maximum(array, -reach), reach).astype(held_as)


def setup_inputs(seed: int = 0) -> dict:
    keys = jax.random.split(jax.random.key(seed), 11)
    pressure_start = noise(keys[0], (NX, NY, NZ), 1.0, 6.0, ((0, 2), (1, 4), (2, 4)), jnp.float32)
    saturation = jnp.clip(0.1 + 0.79999997 * jax.random.uniform(keys[1], (NX, NY, NZ), jnp.float32) ** levels(keys[1], (NX, NY, NZ), ((0, 2), (1, 4), (2, 4)), -0.2, 0.2), 0.1, 0.9)
    permeability = jnp.clip(jnp.exp(math.log(10.0) - 4.6051702 * jax.random.uniform(keys[2], (NX, NY, NZ), jnp.float32) ** levels(keys[2], (NX, NY, NZ), ((0, 2), (1, 4), (2, 4)), -0.2, 0.2)), 0.1, 10.0)
    rock_type = set_ends(jax.random.randint(keys[3], (NX, NY, NZ), 0, ROCKS), jax.random.fold_in(keys[3], 1), 0, ROCKS - 1).astype(jnp.int32)
    rock_table = jnp.clip(jax.random.uniform(keys[4], (5, ROCKS), jnp.float32, 0.5, 3.0), 0.5, 3.0)
    well_cells = set_ends(jax.random.randint(keys[5], (WELLS,), 0, NX * NY * NZ), jax.random.fold_in(keys[5], 1), 0, (NX * NY * NZ) - 1).astype(jnp.int32)
    well_rates = noise(keys[6], (WELLS,), 3.0, 12.0, (), jnp.float32)
    owner_map_keys = jax.random.split(jax.random.fold_in(keys[7], 1), SLABS_X * SLABS_Y * LAYERS_Z * BRICKS // BRICKS)
    owner_map_turns = jax.random.permutation(jax.random.fold_in(keys[7], 3), SLABS_X * SLABS_Y * LAYERS_Z * BRICKS // BRICKS)
    owner_map = jax.vmap(lambda own, number: assign_block(jax.random.fold_in(keys[7], 2), own, number, BRICKS, SLABS_X, 1, CAP, 2))(owner_map_keys, owner_map_turns).reshape((SLABS_X, SLABS_Y, LAYERS_Z, BRICKS, 1))
    stiffness = draw_stiffness(jax.random.fold_in(keys[10], 71), 0)
    anchored = set_ends((jax.random.randint(keys[9], (NX, NY, NZ), 0, 24) < 1).astype(jnp.int32), jax.random.fold_in(keys[9], 1), 0, 1)
    return {"pressure_start": pressure_start, "saturation": saturation, "permeability": permeability, "rock_type": rock_type, "rock_table": rock_table, "well_cells": well_cells, "well_rates": well_rates, "owner_map": owner_map, "stiffness": stiffness, "anchored": anchored}


OMEGA = 0.6
OFFSETS = tuple((along_x, along_y, along_z) for along_x in (0, 1) for along_y in (0, 1) for along_z in (0, 1))


def corner_signs():
    sign_table = np.zeros((24,), np.float32)
    for comp_idx in range(3):
        for corner_idx, offset in enumerate(OFFSETS):
            sign_table[comp_idx * 8 + corner_idx] = 0.25 * (2 * offset[comp_idx] - 1)
    return jnp.asarray(sign_table)


def rock_values(rock_type, rock_table):
    rock_ids = jnp.arange(rock_table.shape[1], dtype=jnp.int32)
    one_hot = (rock_type[None] == rock_ids[:, None, None, None]).astype(jnp.float32)
    return jnp.tensordot(rock_table, one_hot, 1, precision=lax.Precision.HIGHEST)


def transmit(left_value, right_value):
    summed = left_value + right_value
    return 2.0 * left_value * right_value / jnp.where(summed > 0, summed, 1.0)


def neighbour_view(values, axis_dim, shift_by):
    starts = [1, 1, 1]
    starts[axis_dim] = 1 + shift_by
    finish = [starts[0] + values.shape[0] - 2, starts[1] + values.shape[1] - 2, starts[2] + values.shape[2] - 2]
    return lax.slice(values, starts, finish)


def relax_cells(padded_p, padded_k, numerator, denominator):
    centre = padded_k[1:-1, 1:-1, 1:-1]
    total_num = numerator
    total_den = denominator
    for axis_dim in range(3):
        for shift_by in (-1, 1):
            trans = transmit(centre, neighbour_view(padded_k, axis_dim, shift_by))
            total_num = total_num + trans * neighbour_view(padded_p, axis_dim, shift_by)
            total_den = total_den + trans
    return total_num / total_den


def pad_cells(values):
    values = jnp.pad(values, ((1, 1), (0, 0), (0, 0)), mode="wrap")
    return jnp.pad(values, ((0, 0), (1, 1), (1, 1)))


def gather_nodes(nodes):
    pieces = []
    for offset in OFFSETS:
        rolled = jnp.roll(nodes, -offset[0], axis=1)
        pieces.append(rolled[:, :, offset[1]:offset[1] + NY, offset[2]:offset[2] + NZ])
    stacked = jnp.stack(pieces, axis=1)
    return stacked.reshape((stacked.shape[0] * 8,) + stacked.shape[2:])


def spread_nodes(element):
    comps = element.shape[0] // 8
    shaped = element.reshape((comps, 8) + element.shape[1:])
    summed = jnp.zeros((comps, NX, NY + 1, NZ + 1), jnp.float32)
    for corner_idx, offset in enumerate(OFFSETS):
        padded = jnp.pad(shaped[:, corner_idx], ((0, 0), (0, 0), (offset[1], 1 - offset[1]), (offset[2], 1 - offset[2])))
        summed = summed + jnp.roll(padded, offset[0], axis=1)
    return summed


def brick_blocks(owner_map, stiffness):
    owners = owner_map[..., 0]
    one_hot = (owners[..., None] == jnp.arange(N_GX, dtype=jnp.int32)).astype(jnp.int32)
    before = jnp.cumsum(one_hot, axis=3) - one_hot
    brick_rank = jnp.sum(before * one_hot, axis=-1).astype(jnp.int32)
    source_x = jnp.arange(N_GX, dtype=jnp.int32)[:, None, None, None]
    index_y = jnp.arange(N_GY, dtype=jnp.int32)[None, :, None, None]
    index_z = jnp.arange(N_GRP, dtype=jnp.int32)[None, None, :, None]
    picked = stiffness[owners, index_y, index_z, source_x, brick_rank]
    picked = picked.reshape(N_GX, N_GY, N_GRP, CX, CY, 24, 24)
    picked = picked.transpose(0, 3, 1, 4, 2, 5, 6)
    return picked.reshape(NX, NY, N_GRP, 24, 24)


def element_products(blocks, rounded):
    shaped = rounded.reshape(24, NX, NY, N_GRP, CZ).transpose(1, 2, 3, 0, 4).astype(jnp.float32)
    result = jnp.einsum("xygrc,xygcz->xygrz", blocks.astype(jnp.float32), shaped, precision=lax.Precision.HIGHEST)
    return result.transpose(3, 0, 1, 2, 4).reshape(24, NX, NY, NZ)


def reference(pressure_start, saturation, permeability, rock_type, rock_table, well_cells, well_rates, owner_map, stiffness, anchored):
    rock_props = rock_values(rock_type, rock_table)
    mobility = jnp.exp(rock_props[0] * jnp.log(saturation)) + 2.0 * jnp.exp(rock_props[1] * jnp.log(1.0 - saturation))
    conductance = permeability * mobility
    storage = rock_props[2]
    stress_term = rock_props[3]
    biot_coef = rock_props[4]
    source = jnp.zeros((NX * NY * NZ,), jnp.float32).at[well_cells].add(well_rates).reshape(NX, NY, NZ)
    base_term = storage * pressure_start + source
    padded_k = pad_cells(conductance)
    blocks = brick_blocks(owner_map, stiffness)
    diag_brick = jnp.diagonal(blocks.astype(jnp.float32), axis1=3, axis2=4)
    diag_elem = jnp.broadcast_to(diag_brick.transpose(3, 0, 1, 2)[..., None], (24, NX, NY, N_GRP, CZ)).reshape(24, NX, NY, NZ)
    node_diag = spread_nodes(diag_elem)
    anchor_elem = jnp.broadcast_to(anchored.astype(jnp.float32)[None], (8, NX, NY, NZ))
    free_nodes = jnp.where(spread_nodes(anchor_elem) > 0, 0.0, 1.0).astype(jnp.float32)
    corner_sign = corner_signs()
    displacement = jnp.zeros((3, NX, NY + 1, NZ + 1), jnp.float32)
    strain = jnp.zeros((NX, NY, NZ), jnp.float32)
    pressure = pressure_start
    for outer_step in range(ITERS):
        anchor = pressure
        numerator = base_term + stress_term * anchor - biot_coef * strain
        denominator = storage + stress_term
        for flow_step in range(FLOW_PASSES):
            pressure = relax_cells(pad_cells(pressure), padded_k, numerator, denominator)
        biot_load = (biot_coef * pressure)[None] * corner_sign[:, None, None, None]
        for mech_step in range(MECH_PASSES):
            corner_u = gather_nodes(displacement)
            rounded = corner_u.astype(jnp.bfloat16)
            element_force = element_products(blocks, rounded)
            residual = spread_nodes(biot_load - element_force)
            displacement = free_nodes * (displacement + OMEGA * residual / node_diag)
        strain = jnp.tensordot(corner_sign, gather_nodes(displacement), 1, precision=lax.Precision.HIGHEST)
    return pressure, strain
```

```python
import functools

import jax
import jax.numpy as jnp
import numpy as np
from jax import lax
from jax.experimental import pallas as pl
from jax.experimental.pallas import tpu as pltpu
from jax.sharding import PartitionSpec as P

ITERS = 2
FLOW_PASSES = 4
MECH_PASSES = 3
OMEGA = 0.6
MESH = pl.DeviceIdType.MESH


def corner_maps(cells_y):
    rows = np.zeros((4, 8, 24), np.float32)
    lines = cells_y + 1
    cols = np.zeros((cells_y, 24, 2 * lines * 8), np.float32)
    for comp in range(3):
        for dx in (0, 1):
            for dy in (0, 1):
                for dz in (0, 1):
                    entry = 8 * comp + 4 * dx + 2 * dy + dz
                    rows[2 * dx + dy, 4 * dz + comp, entry] = 1.0
                    for k in range(cells_y):
                        cols[k, entry, dx * lines * 8 + (k + dy) * 8 + 4 * dz + comp] = 1.0
    return rows, cols


def brick_blocks(owner_map, stiffness, count_x, bricks):
    owners = owner_map.reshape(-1)
    capacity = stiffness.shape[4]
    one_hot = (owners[:, None] == jnp.arange(count_x, dtype=jnp.int32)[None, :]).astype(jnp.int32)
    before = jnp.cumsum(one_hot, axis=0) - one_hot
    brick_rank = jnp.sum(before * one_hot, axis=1)
    slot_index = owners * capacity + brick_rank
    held_blocks = stiffness.reshape(count_x, capacity, 24, 24)
    fetched = lax.all_to_all(held_blocks, "gx", split_axis=0, concat_axis=0, tiled=True)
    return fetched.reshape(count_x * capacity, 24, 24)[slot_index]


def kernel(
    axes,
    table_ref,
    cells_ref,
    rates_ref,
    p0_ref,
    sat_ref,
    perm_ref,
    rock_ref,
    anch_ref,
    big_ref,
    diag_ref,
    p_out,
    s_out,
    p,
    cond,
    base,
    stress,
    biot,
    numer,
    inv_den,
    trans,
    bload,
    strain,
    disp,
    res,
    load,
    free,
    gain,
    y_send,
    z_send,
    x_recv,
    y_recv,
    z_recv,
    nz_send,
    nx_recv,
    ny_recv,
    nz_recv,
    fs_sem,
    fr_sem,
    ns_sem,
    nr_sem,
):
    count_x, count_y, count_z = axes
    cx, cy, cz = p0_ref.shape
    gx, gy, gz = lax.axis_index("gx"), lax.axis_index("gy"), lax.axis_index("grp")
    x_lo, x_hi = lax.rem(gx + count_x - 1, count_x), lax.rem(gx + 1, count_x)
    y_lo, y_hi = lax.max(gy - 1, 0), lax.min(gy + 1, count_y - 1)
    z_lo, z_hi = lax.max(gz - 1, 0), lax.min(gz + 1, count_z - 1)
    has = {
        ("gx", 0): None,
        ("gx", 1): None,
        ("gy", 0): gy > 0,
        ("gy", 1): gy < count_y - 1,
        ("grp", 0): gz > 0,
        ("grp", 1): gz < count_z - 1,
    }
    peer = {
        ("gx", 0): x_lo,
        ("gx", 1): x_hi,
        ("gy", 0): y_lo,
        ("gy", 1): y_hi,
        ("grp", 0): z_lo,
        ("grp", 1): z_hi,
    }

    def when(key, act):
        if has[key] is None:
            act()
        else:
            pl.when(has[key])(act)

    y_recv[...] = jnp.zeros_like(y_recv)
    z_recv[...] = jnp.zeros_like(z_recv)
    ny_recv[...] = jnp.zeros_like(ny_recv)
    nz_recv[...] = jnp.zeros_like(nz_recv)
    barrier = pltpu.get_barrier_semaphore()
    for key in peer:
        when(
            key,
            lambda key=key: pl.semaphore_signal(
                barrier, inc=1, device_id={key[0]: peer[key]}, device_id_type=MESH
            ),
        )

    rock = rock_ref[...]

    def rock_row(row):
        value = jnp.full(rock.shape, table_ref[row, 0], jnp.float32)
        for kind in range(1, table_ref.shape[1]):
            value = jnp.where(rock == kind, table_ref[row, kind], value)
        return value

    sat = sat_ref[...]
    cond[...] = perm_ref[...] * (
        jnp.exp(rock_row(0) * jnp.log(sat)) + 2.0 * jnp.exp(rock_row(1) * jnp.log(1.0 - sat))
    )
    p[...] = p0_ref[...]

    peers = 2
    for test in has.values():
        if test is not None:
            peers = peers + test.astype(jnp.int32)
    pl.semaphore_wait(barrier, peers)

    lane2 = lax.broadcasted_iota(jnp.int32, (cy, cz), 1)

    def exchange(copies):
        for axis, side, copy in copies:
            when((axis, side), copy.start)
        return copies

    def finish(copies):
        for axis, side, copy in copies:
            when((axis, side), copy.wait_send)
            when((axis, 1 - side), copy.wait_recv)

    def remote(axis, side, src, dst, send_sem, recv_sem):
        return (
            axis,
            side,
            pltpu.make_async_remote_copy(
                src_ref=src,
                dst_ref=dst,
                send_sem=send_sem,
                recv_sem=recv_sem,
                device_id={axis: peer[(axis, side)]},
                device_id_type=MESH,
            ),
        )

    def face_start(field, slot):
        for i in range(cx):
            y_send[slot, 0, i : i + 1, :] = field[i, 0:1, :]
            y_send[slot, 1, i : i + 1, :] = field[i, cy - 1 : cy, :]
        packed = jnp.zeros((cy, cz), jnp.float32)
        for i in range(cx):
            plane = field[i]
            packed = jnp.where(lane2 == i, pltpu.roll(plane, i, 1) if i else plane, packed)
            packed = jnp.where(lane2 == cx + i, pltpu.roll(plane, cx + i + 1, 1), packed)
        z_send[slot] = packed
        copies = []
        for side in (0, 1):
            at = 1 - side
            copies.append(
                remote(
                    "grp", side, z_send.at[slot], z_recv.at[slot, at],
                    fs_sem.at[slot, side], fr_sem.at[slot, at],
                )
            )
            copies.append(
                remote(
                    "gy", side, y_send.at[slot, side], y_recv.at[slot, at],
                    fs_sem.at[slot, 2 + side], fr_sem.at[slot, 2 + at],
                )
            )
            copies.append(
                remote(
                    "gx", side, field.at[side * (cx - 1)], x_recv.at[slot, at],
                    fs_sem.at[slot, 4 + side], fr_sem.at[slot, 4 + at],
                )
            )
        return exchange(copies)

    lane3 = lax.broadcasted_iota(jnp.int32, (cx, cy, cz), 2)
    sub3 = lax.broadcasted_iota(jnp.int32, (cx, cy, cz), 1)

    def views(field, slot):
        value = field[...]
        z_left = z_recv[slot, 0]
        z_right = z_recv[slot, 1]
        from_left = jnp.stack([pltpu.roll(z_left, cz - cx - i, 1) for i in range(cx)])
        from_right = jnp.stack([pltpu.roll(z_right, cz - 1 - i, 1) for i in range(cx)])
        y_left = jnp.stack(
            [jnp.broadcast_to(y_recv[slot, 0, i : i + 1, :], (cy, cz)) for i in range(cx)]
        )
        y_right = jnp.stack(
            [jnp.broadcast_to(y_recv[slot, 1, i : i + 1, :], (cy, cz)) for i in range(cx)]
        )
        return (
            jnp.concatenate([x_recv[slot, 0][None], value[:-1]], axis=0),
            jnp.concatenate([value[1:], x_recv[slot, 1][None]], axis=0),
            jnp.where(sub3 == 0, y_left, pltpu.roll(value, 1, 1)),
            jnp.where(sub3 == cy - 1, y_right, pltpu.roll(value, cy - 1, 1)),
            jnp.where(lane3 == 0, from_left, pltpu.roll(value, 1, 2)),
            jnp.where(lane3 == cz - 1, from_right, pltpu.roll(value, cz - 1, 2)),
        )

    cond_copies = face_start(cond, 0)

    storage = rock_row(2)
    stress[...] = rock_row(3)
    biot[...] = rock_row(4)
    plane_size = cy * count_y * cz * count_z
    flat = (
        (lax.broadcasted_iota(jnp.int32, (cx, cy, cz), 0) + gx * cx) * plane_size
        + (sub3 + gy * cy) * (cz * count_z)
        + lane3
        + gz * cz
    )

    def add_well(well, source):
        return source + jnp.where(flat == cells_ref[well], rates_ref[well], 0.0)

    source = lax.fori_loop(
        0, cells_ref.shape[0], add_well, jnp.zeros((cx, cy, cz), jnp.float32)
    )
    base[...] = storage * p0_ref[...] + source

    row = lax.broadcasted_iota(jnp.int32, (8, cz), 0)
    lane = lax.broadcasted_iota(jnp.int32, (8, cz), 1)
    comp = lax.rem(row, 4)
    along_z = row >= 4
    signs = {}
    for dx in (0, 1):
        for dy in (0, 1):
            signs[dx, dy] = jnp.where(
                comp == 0,
                0.25 * (2 * dx - 1),
                jnp.where(
                    comp == 1,
                    0.25 * (2 * dy - 1),
                    jnp.where(comp == 2, jnp.where(along_z, 0.25, -0.25), 0.0),
                ),
            )

    def share(slot):
        first = jnp.zeros((8, cz), jnp.float32)
        second = jnp.zeros((8, cz), jnp.float32)
        for x in range(cx + 1):
            for y in range(cy + 1):
                n = x * (cy + 1) + y
                line = res[x, y]
                first = jnp.where(lane == n, pltpu.roll(line, n, 1) if n else line, first)
                second = jnp.where(lane == n, pltpu.roll(line, n + 1, 1), second)
        nz_send[slot] = jnp.where(along_z, second, first)
        finish(
            exchange(
                [
                    remote(
                        "grp", side, nz_send.at[slot], nz_recv.at[slot, 1 - side],
                        ns_sem.at[slot, side], nr_sem.at[slot, 1 - side],
                    )
                    for side in (0, 1)
                ]
            )
        )
        beside = pltpu.roll(jnp.where(along_z, nz_recv[slot, 0], nz_recv[slot, 1]), 4, 0)
        for x in range(cx + 1):
            for y in range(cy + 1):
                n = x * (cy + 1) + y
                line = res[x, y]
                swapped = pltpu.roll(line, 4, 0)
                low = jnp.where(
                    lane == 0, pltpu.roll(beside, cz - n, 1) if n else beside, pltpu.roll(swapped, 1, 1)
                )
                high = jnp.where(
                    lane == cz - 1, pltpu.roll(beside, cz - 1 - n, 1), pltpu.roll(swapped, cz - 1, 1)
                )
                res[x, y] = line + jnp.where(along_z, high, low)
        finish(
            exchange(
                [
                    remote(
                        "gy", side, res.at[:, side * cy], ny_recv.at[slot, 1 - side],
                        ns_sem.at[slot, 2 + side], nr_sem.at[slot, 2 + 1 - side],
                    )
                    for side in (0, 1)
                ]
            )
        )
        for x in range(cx + 1):
            res[x, 0] = res[x, 0] + ny_recv[slot, 0, x]
            res[x, cy] = res[x, cy] + ny_recv[slot, 1, x]
        finish(
            exchange(
                [
                    remote(
                        "gx", side, res.at[side * cx], nx_recv.at[slot, 1 - side],
                        ns_sem.at[slot, 4 + side], nr_sem.at[slot, 4 + 1 - side],
                    )
                    for side in (0, 1)
                ]
            )
        )
        res[0] = res[0] + nx_recv[slot, 0]
        res[cx] = res[cx] + nx_recv[slot, 1]

    for x in range(cx + 1):
        for y in range(cy + 1):
            total = jnp.zeros((8, cz), jnp.float32)
            for dx in (0, 1):
                for dy in (0, 1):
                    i, k = x - dx, y - dy
                    if 0 <= i < cx and 0 <= k < cy:
                        held = jnp.broadcast_to(
                            anch_ref[i, k : k + 1, :].astype(jnp.float32), (8, cz)
                        )
                        total = total + jnp.where(comp == 3, held, diag_ref[i, k, 2 * dx + dy])
            res[x, y] = total
    share(0)
    for x in range(cx + 1):
        for y in range(cy + 1):
            line = res[x, y]
            count = jnp.where(along_z, line[7:8, :], line[3:4, :])
            keep = jnp.where((count > 0) | (comp == 3), 0.0, 1.0)
            free[x, y] = keep
            gain[x, y] = keep * OMEGA / jnp.where(comp == 3, 1.0, line)
    disp[...] = jnp.zeros_like(disp)
    strain[...] = jnp.zeros_like(strain)

    finish(cond_copies)
    centre = cond[...]
    total_den = storage + stress[...]
    for at, other in enumerate(views(cond, 0)):
        link = 2.0 * centre * other / (centre + other)
        trans[at] = link
        total_den = total_den + link
    inv_den[...] = 1.0 / total_den

    def outer(step, carry):
        numer[...] = base[...] + stress[...] * p[...] - biot[...] * strain[...]

        def flow(turn, carry):
            slot = 1 + step * FLOW_PASSES + turn
            finish(face_start(p, slot))
            total = numer[...]
            for at, other in enumerate(views(p, slot)):
                total = total + trans[at] * other
            p[...] = total * inv_den[...]
            return carry

        lax.fori_loop(0, FLOW_PASSES, flow, 0)
        bload[...] = biot[...] * p[...]
        for x in range(cx + 1):
            for y in range(cy + 1):
                total = jnp.zeros((8, cz), jnp.float32)
                for dx in (0, 1):
                    for dy in (0, 1):
                        i, k = x - dx, y - dy
                        if 0 <= i < cx and 0 <= k < cy:
                            total = total + signs[dx, dy] * jnp.broadcast_to(
                                bload[i, k : k + 1, :], (8, cz)
                            )
                load[x, y] = total

        def mech(turn, carry):
            slot = 1 + step * MECH_PASSES + turn
            res[...] = load[...]
            for i in range(cx):
                pair = disp[i : i + 2].reshape(2 * (cy + 1) * 8, cz).astype(jnp.bfloat16)
                force = jnp.dot(big_ref[i], pair, preferred_element_type=jnp.float32)
                force = force.reshape(4, cy, 8, cz)
                res[i, 0:cy] = res[i, 0:cy] - force[0]
                res[i, 1 : cy + 1] = res[i, 1 : cy + 1] - force[1]
                res[i + 1, 0:cy] = res[i + 1, 0:cy] - force[2]
                res[i + 1, 1 : cy + 1] = res[i + 1, 1 : cy + 1] - force[3]
            share(slot)
            for x in range(cx + 1):
                disp[x] = free[x] * disp[x] + gain[x] * res[x]
            return carry

        lax.fori_loop(0, MECH_PASSES, mech, 0)
        for i in range(cx):
            for k in range(cy):
                total = jnp.zeros((8, cz), jnp.float32)
                for dx in (0, 1):
                    for dy in (0, 1):
                        total = total + signs[dx, dy] * disp[i + dx, k + dy]
                strain[i, k : k + 1, :] = jnp.sum(total, axis=0, keepdims=True)
        return carry

    lax.fori_loop(0, ITERS, outer, 0)
    p_out[...] = p[...]
    s_out[...] = strain[...]


def per_device(
    pressure_start,
    saturation,
    permeability,
    rock_type,
    rock_table,
    well_cells,
    well_rates,
    owner_map,
    stiffness,
    anchored,
):
    cx, cy, cz = pressure_start.shape
    axes = (lax.axis_size("gx"), lax.axis_size("gy"), lax.axis_size("grp"))
    brick_k = brick_blocks(owner_map, stiffness, axes[0], cx * cy)
    rows, cols = corner_maps(cy)
    rows_b, cols_b = jnp.asarray(rows, jnp.bfloat16), jnp.asarray(cols, jnp.bfloat16)
    shaped = brick_k.reshape(cx, cy, 24, 24)
    spread = jnp.einsum(
        "ikrs,ksc->ikrc", shaped, cols_b, preferred_element_type=jnp.float32
    ).astype(jnp.bfloat16)
    big = jnp.einsum(
        "qmr,ikrc->iqkmc", rows_b, spread, preferred_element_type=jnp.float32
    ).astype(jnp.bfloat16)
    big = big.reshape(cx, 4 * cy * 8, cols.shape[2])
    diag = jnp.einsum(
        "qmr,ikr->ikqm",
        rows_b,
        jnp.diagonal(shaped, axis1=2, axis2=3),
        preferred_element_type=jnp.float32,
    )
    diag = jnp.broadcast_to(diag[..., None], (cx, cy, 4, 8, cz))

    cell = (cx, cy, cz)
    line = (cx + 1, cy + 1, 8, cz)
    flows = 1 + ITERS * FLOW_PASSES
    shares = 1 + ITERS * MECH_PASSES
    f32 = jnp.float32
    vmem = pl.BlockSpec(memory_space=pltpu.VMEM)
    smem = pl.BlockSpec(memory_space=pltpu.SMEM)
    return pl.pallas_call(
        functools.partial(kernel, axes),
        out_shape=(jax.ShapeDtypeStruct(cell, f32), jax.ShapeDtypeStruct(cell, f32)),
        in_specs=[smem] * 3 + [vmem] * 7,
        out_specs=(vmem, vmem),
        scratch_shapes=[pltpu.VMEM(cell, f32)] * 7
        + [pltpu.VMEM((6,) + cell, f32)]
        + [pltpu.VMEM(cell, f32)] * 2
        + [pltpu.VMEM(line, f32)] * 5
        + [
            pltpu.VMEM((flows, 2, cx, cz), f32),
            pltpu.VMEM((flows, cy, cz), f32),
            pltpu.VMEM((flows, 2, cy, cz), f32),
            pltpu.VMEM((flows, 2, cx, cz), f32),
            pltpu.VMEM((flows, 2, cy, cz), f32),
            pltpu.VMEM((shares, 8, cz), f32),
            pltpu.VMEM((shares, 2, cy + 1, 8, cz), f32),
            pltpu.VMEM((shares, 2, cx + 1, 8, cz), f32),
            pltpu.VMEM((shares, 2, 8, cz), f32),
            pltpu.SemaphoreType.DMA((flows, 6)),
            pltpu.SemaphoreType.DMA((flows, 6)),
            pltpu.SemaphoreType.DMA((shares, 6)),
            pltpu.SemaphoreType.DMA((shares, 6)),
        ],
        compiler_params=pltpu.CompilerParams(collective_id=0, has_side_effects=True),
    )(
        rock_table,
        well_cells,
        well_rates,
        pressure_start,
        saturation,
        permeability,
        rock_type,
        anchored,
        big,
        diag,
    )


def solution(mesh):
    cells = P("gx", "gy", "grp")
    placed = (
        cells,
        cells,
        cells,
        cells,
        P(),
        P(),
        P(),
        P("gx", "gy", "grp", None, None),
        P("gx", "gy", "grp", None, None, None, None),
        cells,
    )
    return jax.shard_map(
        per_device, mesh=mesh, in_specs=placed, out_specs=(cells, cells), check_vma=False
    )
```

```python
import functools

import jax
import jax.numpy as jnp
import numpy as np
from jax import lax
from jax.experimental import pallas as pl
from jax.experimental.pallas import tpu as pltpu
from jax.sharding import PartitionSpec as P

ITERS = 2
FLOW_PASSES = 4
MECH_PASSES = 3
OMEGA = 0.6
MESH = pl.DeviceIdType.MESH


def corner_maps(cells_y):
    rows = np.zeros((4, 8, 24), np.float32)
    lines = cells_y + 1
    cols = np.zeros((cells_y, 24, 2 * lines * 8), np.float32)
    for comp in range(3):
        for dx in (0, 1):
            for dy in (0, 1):
                for dz in (0, 1):
                    entry = 8 * comp + 4 * dx + 2 * dy + dz
                    rows[2 * dx + dy, 4 * dz + comp, entry] = 1.0
                    for k in range(cells_y):
                        cols[k, entry, dx * lines * 8 + (k + dy) * 8 + 4 * dz + comp] = 1.0
    return rows, cols


def brick_blocks(owner_map, stiffness, count_x, bricks):
    owners = owner_map.reshape(-1)
    capacity = stiffness.shape[4]
    one_hot = (owners[:, None] == jnp.arange(count_x, dtype=jnp.int32)[None, :]).astype(jnp.int32)
    before = jnp.cumsum(one_hot, axis=0) - one_hot
    brick_rank = jnp.sum(before * one_hot, axis=1)
    slot_index = owners * capacity + brick_rank
    held_blocks = stiffness.reshape(count_x, capacity, 24, 24)
    fetched = lax.all_to_all(held_blocks, "gx", split_axis=0, concat_axis=0, tiled=True)
    return fetched.reshape(count_x * capacity, 24, 24)[slot_index]


def kernel(
    axes,
    table_ref,
    cells_ref,
    rates_ref,
    p0_ref,
    sat_ref,
    perm_ref,
    rock_ref,
    anch_ref,
    big_ref,
    diag_ref,
    p_out,
    s_out,
    p,
    cond,
    base,
    stress,
    biot,
    numer,
    inv_den,
    trans,
    bload,
    strain,
    disp,
    res,
    load,
    free,
    gain,
    y_send,
    z_send,
    x_recv,
    y_recv,
    z_recv,
    nz_send,
    nx_recv,
    ny_recv,
    nc_recv,
    nz_recv,
    fs_sem,
    fr_sem,
    ns_sem,
    nr_sem,
):
    count_x, count_y, count_z = axes
    cx, cy, cz = p0_ref.shape
    gx, gy, gz = lax.axis_index("gx"), lax.axis_index("gy"), lax.axis_index("grp")
    x_lo, x_hi = lax.rem(gx + count_x - 1, count_x), lax.rem(gx + 1, count_x)
    y_lo, y_hi = lax.max(gy - 1, 0), lax.min(gy + 1, count_y - 1)
    z_lo, z_hi = lax.max(gz - 1, 0), lax.min(gz + 1, count_z - 1)
    has = {
        ("gx", 0): None,
        ("gx", 1): None,
        ("gy", 0): gy > 0,
        ("gy", 1): gy < count_y - 1,
        ("grp", 0): gz > 0,
        ("grp", 1): gz < count_z - 1,
    }
    peer = {
        ("gx", 0): x_lo,
        ("gx", 1): x_hi,
        ("gy", 0): y_lo,
        ("gy", 1): y_hi,
        ("grp", 0): z_lo,
        ("grp", 1): z_hi,
    }

    def when(key, act):
        if has[key] is None:
            act()
        else:
            pl.when(has[key])(act)

    def near(shift_y, shift_z):
        tests = [
            test
            for test in (
                {-1: has["gy", 0], 0: None, 1: has["gy", 1]}[shift_y],
                {-1: has["grp", 0], 0: None, 1: has["grp", 1]}[shift_z],
            )
            if test is not None
        ]
        return functools.reduce(jnp.logical_and, tests) if tests else None

    groups = {(sy, sz): near(sy, sz) for sz in (-1, 0, 1) for sy in (-1, 0, 1)}
    at_x, at_y, at_z = (
        {-1: x_lo, 0: gx, 1: x_hi},
        {-1: y_lo, 0: gy, 1: y_hi},
        {-1: z_lo, 0: gz, 1: z_hi},
    )

    def members(group):
        return [(sx,) + group for sx in (-1, 0, 1) if (sx,) + group != (0, 0, 0)]

    def guarded(test, act):
        if test is None:
            act()
        else:
            pl.when(test)(act)

    def device(shift):
        return {"gx": at_x[shift[0]], "gy": at_y[shift[1]], "grp": at_z[shift[2]]}

    y_recv[...] = jnp.zeros_like(y_recv)
    z_recv[...] = jnp.zeros_like(z_recv)
    ny_recv[...] = jnp.zeros_like(ny_recv)
    nc_recv[...] = jnp.zeros_like(nc_recv)
    nz_recv[...] = jnp.zeros_like(nz_recv)
    barrier = pltpu.get_barrier_semaphore()

    def greet(group):
        for shift in members(group):
            pl.semaphore_signal(barrier, inc=1, device_id=device(shift), device_id_type=MESH)

    for group, test in groups.items():
        guarded(test, lambda group=group: greet(group))

    rock = rock_ref[...]

    def rock_row(row):
        value = jnp.full(rock.shape, table_ref[row, 0], jnp.float32)
        for kind in range(1, table_ref.shape[1]):
            value = jnp.where(rock == kind, table_ref[row, kind], value)
        return value

    sat = sat_ref[...]
    cond[...] = perm_ref[...] * (
        jnp.exp(rock_row(0) * jnp.log(sat)) + 2.0 * jnp.exp(rock_row(1) * jnp.log(1.0 - sat))
    )
    p[...] = p0_ref[...]

    def span(axis):
        return 1 + has[axis, 0].astype(jnp.int32) + has[axis, 1].astype(jnp.int32)

    pl.semaphore_wait(barrier, 3 * span("gy") * span("grp") - 1)

    lane2 = lax.broadcasted_iota(jnp.int32, (cy, cz), 1)

    def exchange(copies):
        for axis, side, copy in copies:
            when((axis, side), copy.start)
        return copies

    def finish(copies):
        for axis, side, copy in copies:
            when((axis, side), copy.wait_send)
            when((axis, 1 - side), copy.wait_recv)

    def remote(axis, side, src, dst, send_sem, recv_sem):
        return (
            axis,
            side,
            pltpu.make_async_remote_copy(
                src_ref=src,
                dst_ref=dst,
                send_sem=send_sem,
                recv_sem=recv_sem,
                device_id={axis: peer[(axis, side)]},
                device_id_type=MESH,
            ),
        )

    def face_start(field, slot):
        for i in range(cx):
            y_send[slot, 0, i : i + 1, :] = field[i, 0:1, :]
            y_send[slot, 1, i : i + 1, :] = field[i, cy - 1 : cy, :]
        packed = jnp.zeros((cy, cz), jnp.float32)
        for i in range(cx):
            plane = field[i]
            packed = jnp.where(lane2 == i, pltpu.roll(plane, i, 1) if i else plane, packed)
            packed = jnp.where(lane2 == cx + i, pltpu.roll(plane, cx + i + 1, 1), packed)
        z_send[slot] = packed
        copies = []
        for side in (0, 1):
            at = 1 - side
            copies.append(
                remote(
                    "grp", side, z_send.at[slot], z_recv.at[slot, at],
                    fs_sem.at[slot, side], fr_sem.at[slot, at],
                )
            )
            copies.append(
                remote(
                    "gy", side, y_send.at[slot, side], y_recv.at[slot, at],
                    fs_sem.at[slot, 2 + side], fr_sem.at[slot, 2 + at],
                )
            )
            copies.append(
                remote(
                    "gx", side, field.at[side * (cx - 1)], x_recv.at[slot, at],
                    fs_sem.at[slot, 4 + side], fr_sem.at[slot, 4 + at],
                )
            )
        return exchange(copies)

    lane3 = lax.broadcasted_iota(jnp.int32, (cx, cy, cz), 2)
    sub3 = lax.broadcasted_iota(jnp.int32, (cx, cy, cz), 1)

    def views(field, slot):
        value = field[...]
        z_left = z_recv[slot, 0]
        z_right = z_recv[slot, 1]
        from_left = jnp.stack([pltpu.roll(z_left, cz - cx - i, 1) for i in range(cx)])
        from_right = jnp.stack([pltpu.roll(z_right, cz - 1 - i, 1) for i in range(cx)])
        y_left = jnp.stack(
            [jnp.broadcast_to(y_recv[slot, 0, i : i + 1, :], (cy, cz)) for i in range(cx)]
        )
        y_right = jnp.stack(
            [jnp.broadcast_to(y_recv[slot, 1, i : i + 1, :], (cy, cz)) for i in range(cx)]
        )
        return (
            jnp.concatenate([x_recv[slot, 0][None], value[:-1]], axis=0),
            jnp.concatenate([value[1:], x_recv[slot, 1][None]], axis=0),
            jnp.where(sub3 == 0, y_left, pltpu.roll(value, 1, 1)),
            jnp.where(sub3 == cy - 1, y_right, pltpu.roll(value, cy - 1, 1)),
            jnp.where(lane3 == 0, from_left, pltpu.roll(value, 1, 2)),
            jnp.where(lane3 == cz - 1, from_right, pltpu.roll(value, cz - 1, 2)),
        )

    cond_copies = face_start(cond, 0)
    first_copies = face_start(p, 1)

    storage = rock_row(2)
    stress[...] = rock_row(3)
    biot[...] = rock_row(4)
    plane_size = cy * count_y * cz * count_z
    flat = (
        (lax.broadcasted_iota(jnp.int32, (cx, cy, cz), 0) + gx * cx) * plane_size
        + (sub3 + gy * cy) * (cz * count_z)
        + lane3
        + gz * cz
    )

    def add_well(well, source):
        return source + jnp.where(flat == cells_ref[well], rates_ref[well], 0.0)

    source = lax.fori_loop(
        0, cells_ref.shape[0], add_well, jnp.zeros((cx, cy, cz), jnp.float32)
    )
    base[...] = storage * p0_ref[...] + source

    row = lax.broadcasted_iota(jnp.int32, (8, cz), 0)
    lane = lax.broadcasted_iota(jnp.int32, (8, cz), 1)
    comp = lax.rem(row, 4)
    along_z = row >= 4
    signs = {}
    for dx in (0, 1):
        for dy in (0, 1):
            signs[dx, dy] = jnp.where(
                comp == 0,
                0.25 * (2 * dx - 1),
                jnp.where(
                    comp == 1,
                    0.25 * (2 * dy - 1),
                    jnp.where(comp == 2, jnp.where(along_z, 0.25, -0.25), 0.0),
                ),
            )

    edge = lane == jnp.where(along_z, cz - 1, 0)
    across = lax.rem(lane, cy + 1)
    line_x = {
        -1: lane <= cy,
        0: None,
        1: (lane >= cx * (cy + 1)) & (lane < (cx + 1) * (cy + 1)),
    }
    line_y = {-1: across == 0, 0: None, 1: across == cy}

    def message(slot, shift):
        sx, sy, sz = shift
        code = 9 * (sz + 1) + 3 * (sy + 1) + sx + 1
        if sz:
            src = nz_send.at[slot]
            dst = nz_recv.at[slot, z_place(-sx, -sy, -sz)]
        elif sx and sy:
            src = res.at[(sx + 1) // 2 * cx, (sy + 1) // 2 * cy]
            dst = nc_recv.at[slot, (1 - sx) + (1 - sy) // 2]
        elif sx:
            src = res.at[(sx + 1) // 2 * cx]
            dst = nx_recv.at[slot, (1 - sx) // 2]
        else:
            src = res.at[:, (sy + 1) // 2 * cy]
            dst = ny_recv.at[slot, (1 - sy) // 2]
        return pltpu.make_async_remote_copy(
            src_ref=src,
            dst_ref=dst,
            send_sem=ns_sem.at[slot, code],
            recv_sem=nr_sem.at[slot, 26 - code],
            device_id=device(shift),
            device_id_type=MESH,
        )

    def share_start(slot):
        first = jnp.zeros((8, cz), jnp.float32)
        second = jnp.zeros((8, cz), jnp.float32)
        for x in range(cx + 1):
            for y in range(cy + 1):
                n = x * (cy + 1) + y
                line = res[x, y]
                first = jnp.where(lane == n, pltpu.roll(line, n, 1) if n else line, first)
                second = jnp.where(lane == n, pltpu.roll(line, n + 1, 1), second)
                swapped = pltpu.roll(line, 4, 0)
                moved = jnp.where(along_z, pltpu.roll(swapped, cz - 1, 1), pltpu.roll(swapped, 1, 1))
                res[x, y] = line + jnp.where(edge, 0.0, moved)
        nz_send[slot] = jnp.where(along_z, second, first)

        def go(group):
            for shift in members(group):
                message(slot, shift).start()

        for group, test in groups.items():
            guarded(test, lambda group=group: go(group))

    def share_arrive(slot):
        def arrive(group):
            for sx, sy, sz in members(group):
                message(slot, (-sx, -sy, -sz)).wait_recv()

        for group, test in groups.items():
            guarded(test, lambda group=group: arrive(group))
        sides = []
        for sz in (-1, 1):
            total = jnp.zeros((8, cz), jnp.float32)
            for sx in (-1, 0, 1):
                for sy in (-1, 0, 1):
                    part = nz_recv[slot, z_place(sx, sy, sz)]
                    turn = (sx * cx * (cy + 1) + sy * cy) % cz
                    part = pltpu.roll(part, turn, 1) if turn else part
                    for test in (line_x[sx], line_y[sy]):
                        if test is not None:
                            part = jnp.where(test, part, 0.0)
                    total = total + part
            sides.append(total)
        return pltpu.roll(jnp.where(along_z, sides[0], sides[1]), 4, 0)

    def z_place(sx, sy, sz):
        return 9 * (sz + 1) // 2 + 3 * (sy + 1) + sx + 1

    def share_line(slot, beside, x, y):
        n = x * (cy + 1) + y
        total = res[x, y] + jnp.where(edge, jnp.broadcast_to(beside[:, n : n + 1], (8, cz)), 0.0)
        if x in (0, cx):
            total = total + nx_recv[slot, x // cx, y]
        if y in (0, cy):
            total = total + ny_recv[slot, y // cy, x]
        if x in (0, cx) and y in (0, cy):
            total = total + nc_recv[slot, 2 * (x // cx) + y // cy]
        return total

    def share_end(slot):
        def sent(group):
            for shift in members(group):
                message(slot, shift).wait_send()

        for group, test in groups.items():
            guarded(test, lambda group=group: sent(group))

    for x in range(cx + 1):
        for y in range(cy + 1):
            total = jnp.zeros((8, cz), jnp.float32)
            for dx in (0, 1):
                for dy in (0, 1):
                    i, k = x - dx, y - dy
                    if 0 <= i < cx and 0 <= k < cy:
                        held = jnp.broadcast_to(
                            anch_ref[i, k : k + 1, :].astype(jnp.float32), (8, cz)
                        )
                        total = total + jnp.where(comp == 3, held, diag_ref[i, k, 2 * dx + dy])
            res[x, y] = total
    share_start(0)
    disp[...] = jnp.zeros_like(disp)
    strain[...] = jnp.zeros_like(strain)

    finish(cond_copies)
    centre = cond[...]
    total_den = storage + stress[...]
    for at, other in enumerate(views(cond, 0)):
        link = 2.0 * centre * other / (centre + other)
        trans[at] = link
        total_den = total_den + link
    inv_den[...] = 1.0 / total_den

    def relax(slot):
        total = numer[...]
        for at, other in enumerate(views(p, slot)):
            total = total + trans[at] * other
        p[...] = total * inv_den[...]

    def settle(slot):
        share_start(slot)
        beside = share_arrive(slot)
        for x in range(cx + 1):
            for y in range(cy + 1):
                total = share_line(slot, beside, x, y)
                disp[x, y] = free[x, y] * disp[x, y] + gain[x, y] * total
        share_end(slot)

    for step in range(ITERS):
        numer[...] = base[...] + stress[...] * p[...] - biot[...] * strain[...]

        def flow(turn, carry):
            slot = 1 + step * FLOW_PASSES + turn
            finish(face_start(p, slot))
            relax(slot)
            return carry

        if step == 0:
            finish(first_copies)
            relax(1)
        lax.fori_loop(1 if step == 0 else 0, FLOW_PASSES, flow, 0)
        if step == 0:
            beside = share_arrive(0)
            for x in range(cx + 1):
                for y in range(cy + 1):
                    line = share_line(0, beside, x, y)
                    count = jnp.where(along_z, line[7:8, :], line[3:4, :])
                    keep = jnp.where((count > 0) | (comp == 3), 0.0, 1.0)
                    free[x, y] = keep
                    gain[x, y] = keep * OMEGA / jnp.where(comp == 3, 1.0, line)
            share_end(0)
        bload[...] = biot[...] * p[...]
        for x in range(cx + 1):
            for y in range(cy + 1):
                total = jnp.zeros((8, cz), jnp.float32)
                for dx in (0, 1):
                    for dy in (0, 1):
                        i, k = x - dx, y - dy
                        if 0 <= i < cx and 0 <= k < cy:
                            total = total + signs[dx, dy] * jnp.broadcast_to(
                                bload[i, k : k + 1, :], (8, cz)
                            )
                load[x, y] = total

        def mech(turn, carry):
            slot = 1 + step * MECH_PASSES + turn
            res[...] = load[...]
            for i in range(cx):
                pair = disp[i : i + 2].reshape(2 * (cy + 1) * 8, cz).astype(jnp.bfloat16)
                force = jnp.dot(big_ref[i], pair, preferred_element_type=jnp.float32)
                force = force.reshape(4, cy, 8, cz)
                res[i, 0:cy] = res[i, 0:cy] - force[0]
                res[i, 1 : cy + 1] = res[i, 1 : cy + 1] - force[1]
                res[i + 1, 0:cy] = res[i + 1, 0:cy] - force[2]
                res[i + 1, 1 : cy + 1] = res[i + 1, 1 : cy + 1] - force[3]
            settle(slot)
            return carry

        if step == 0:
            res[...] = load[...]
            settle(1)
        lax.fori_loop(1 if step == 0 else 0, MECH_PASSES, mech, 0)
        for i in range(cx):
            for k in range(cy):
                total = jnp.zeros((8, cz), jnp.float32)
                for dx in (0, 1):
                    for dy in (0, 1):
                        total = total + signs[dx, dy] * disp[i + dx, k + dy]
                strain[i, k : k + 1, :] = jnp.sum(total, axis=0, keepdims=True)

    p_out[...] = p[...]
    s_out[...] = strain[...]


def per_device(
    pressure_start,
    saturation,
    permeability,
    rock_type,
    rock_table,
    well_cells,
    well_rates,
    owner_map,
    stiffness,
    anchored,
):
    cx, cy, cz = pressure_start.shape
    axes = (lax.axis_size("gx"), lax.axis_size("gy"), lax.axis_size("grp"))
    brick_k = brick_blocks(owner_map, stiffness, axes[0], cx * cy)
    rows, cols = corner_maps(cy)
    rows_b, cols_b = jnp.asarray(rows, jnp.bfloat16), jnp.asarray(cols, jnp.bfloat16)
    shaped = brick_k.reshape(cx, cy, 24, 24)
    spread = jnp.einsum(
        "ikrs,ksc->ikrc", shaped, cols_b, preferred_element_type=jnp.float32
    ).astype(jnp.bfloat16)
    big = jnp.einsum(
        "qmr,ikrc->iqkmc", rows_b, spread, preferred_element_type=jnp.float32
    ).astype(jnp.bfloat16)
    big = big.reshape(cx, 4 * cy * 8, cols.shape[2])
    diag = jnp.einsum(
        "qmr,ikr->ikqm",
        rows_b,
        jnp.diagonal(shaped, axis1=2, axis2=3),
        preferred_element_type=jnp.float32,
    )
    diag = jnp.broadcast_to(diag[..., None], (cx, cy, 4, 8, cz))

    cell = (cx, cy, cz)
    line = (cx + 1, cy + 1, 8, cz)
    flows = 1 + ITERS * FLOW_PASSES
    shares = 1 + ITERS * MECH_PASSES
    f32 = jnp.float32
    vmem = pl.BlockSpec(memory_space=pltpu.VMEM)
    smem = pl.BlockSpec(memory_space=pltpu.SMEM)
    return pl.pallas_call(
        functools.partial(kernel, axes),
        out_shape=(jax.ShapeDtypeStruct(cell, f32), jax.ShapeDtypeStruct(cell, f32)),
        in_specs=[smem] * 3 + [vmem] * 7,
        out_specs=(vmem, vmem),
        scratch_shapes=[pltpu.VMEM(cell, f32)] * 7
        + [pltpu.VMEM((6,) + cell, f32)]
        + [pltpu.VMEM(cell, f32)] * 2
        + [pltpu.VMEM(line, f32)] * 5
        + [
            pltpu.VMEM((flows, 2, cx, cz), f32),
            pltpu.VMEM((flows, cy, cz), f32),
            pltpu.VMEM((flows, 2, cy, cz), f32),
            pltpu.VMEM((flows, 2, cx, cz), f32),
            pltpu.VMEM((flows, 2, cy, cz), f32),
            pltpu.VMEM((shares, 8, cz), f32),
            pltpu.VMEM((shares, 2, cy + 1, 8, cz), f32),
            pltpu.VMEM((shares, 2, cx + 1, 8, cz), f32),
            pltpu.VMEM((shares, 4, 8, cz), f32),
            pltpu.VMEM((shares, 18, 8, cz), f32),
            pltpu.SemaphoreType.DMA((flows, 6)),
            pltpu.SemaphoreType.DMA((flows, 6)),
            pltpu.SemaphoreType.DMA((shares, 27)),
            pltpu.SemaphoreType.DMA((shares, 27)),
        ],
        compiler_params=pltpu.CompilerParams(collective_id=0, has_side_effects=True),
    )(
        rock_table,
        well_cells,
        well_rates,
        pressure_start,
        saturation,
        permeability,
        rock_type,
        anchored,
        big,
        diag,
    )


def solution(mesh):
    cells = P("gx", "gy", "grp")
    placed = (
        cells,
        cells,
        cells,
        cells,
        P(),
        P(),
        P(),
        P("gx", "gy", "grp", None, None),
        P("gx", "gy", "grp", None, None, None, None),
        cells,
    )
    return jax.shard_map(
        per_device, mesh=mesh, in_specs=placed, out_specs=(cells, cells), check_vma=False
    )
```

```python
import functools

import jax
import jax.numpy as jnp
import numpy as np
from jax import lax
from jax.experimental import pallas as pl
from jax.experimental.pallas import tpu as pltpu
from jax.sharding import PartitionSpec as P

ITERS = 2
FLOW_PASSES = 4
MECH_PASSES = 3
OMEGA = 0.6
MESH = pl.DeviceIdType.MESH


def corner_maps(cells_y):
    rows = np.zeros((4, 8, 24), np.float32)
    lines = cells_y + 1
    cols = np.zeros((cells_y, 24, 2 * lines * 8), np.float32)
    for comp in range(3):
        for dx in (0, 1):
            for dy in (0, 1):
                for dz in (0, 1):
                    entry = 8 * comp + 4 * dx + 2 * dy + dz
                    rows[2 * dx + dy, 4 * dz + comp, entry] = 1.0
                    for k in range(cells_y):
                        cols[k, entry, dx * lines * 8 + (k + dy) * 8 + 4 * dz + comp] = 1.0
    return rows, cols


def brick_blocks(owner_map, stiffness, count_x, bricks):
    owners = owner_map.reshape(-1)
    capacity = stiffness.shape[4]
    one_hot = (owners[:, None] == jnp.arange(count_x, dtype=jnp.int32)[None, :]).astype(jnp.int32)
    before = jnp.cumsum(one_hot, axis=0) - one_hot
    brick_rank = jnp.sum(before * one_hot, axis=1)
    slot_index = owners * capacity + brick_rank
    held_blocks = stiffness.reshape(count_x, capacity, 24, 24)
    fetched = lax.all_to_all(held_blocks, "gx", split_axis=0, concat_axis=0, tiled=True)
    return fetched.reshape(count_x * capacity, 24, 24)[slot_index]


def kernel(
    axes,
    table_ref,
    cells_ref,
    rates_ref,
    p0_ref,
    sat_ref,
    perm_ref,
    rock_ref,
    anch_ref,
    big_ref,
    p_out,
    s_out,
    diag_ref,
    p,
    cond,
    base,
    stress,
    biot,
    numer,
    inv_den,
    trans,
    bload,
    strain,
    disp,
    res,
    load,
    free,
    gain,
    y_send,
    z_send,
    x_recv,
    y_recv,
    z_recv,
    nz_send,
    nx_recv,
    ny_recv,
    nc_recv,
    nz_recv,
    fs_sem,
    fr_sem,
    ns_sem,
    nr_sem,
):
    count_x, count_y, count_z = axes
    cx, cy, cz = p0_ref.shape
    gx, gy, gz = lax.axis_index("gx"), lax.axis_index("gy"), lax.axis_index("grp")
    x_lo, x_hi = lax.rem(gx + count_x - 1, count_x), lax.rem(gx + 1, count_x)
    y_lo, y_hi = lax.max(gy - 1, 0), lax.min(gy + 1, count_y - 1)
    z_lo, z_hi = lax.max(gz - 1, 0), lax.min(gz + 1, count_z - 1)
    has = {
        ("gx", 0): None,
        ("gx", 1): None,
        ("gy", 0): gy > 0,
        ("gy", 1): gy < count_y - 1,
        ("grp", 0): gz > 0,
        ("grp", 1): gz < count_z - 1,
    }
    peer = {
        ("gx", 0): x_lo,
        ("gx", 1): x_hi,
        ("gy", 0): y_lo,
        ("gy", 1): y_hi,
        ("grp", 0): z_lo,
        ("grp", 1): z_hi,
    }

    def when(key, act):
        if has[key] is None:
            act()
        else:
            pl.when(has[key])(act)

    def near(shift_y, shift_z):
        tests = [
            test
            for test in (
                {-1: has["gy", 0], 0: None, 1: has["gy", 1]}[shift_y],
                {-1: has["grp", 0], 0: None, 1: has["grp", 1]}[shift_z],
            )
            if test is not None
        ]
        return functools.reduce(jnp.logical_and, tests) if tests else None

    groups = {(sy, sz): near(sy, sz) for sz in (-1, 0, 1) for sy in (-1, 0, 1)}
    at_x, at_y, at_z = (
        {-1: x_lo, 0: gx, 1: x_hi},
        {-1: y_lo, 0: gy, 1: y_hi},
        {-1: z_lo, 0: gz, 1: z_hi},
    )

    def members(group):
        sides = (-1, 0) if group[1] and count_x == 2 else (-1, 0, 1)
        return [(sx,) + group for sx in sides if (sx,) + group != (0, 0, 0)]

    def guarded(test, act):
        if test is None:
            act()
        else:
            pl.when(test)(act)

    def device(shift):
        return {"gx": at_x[shift[0]], "gy": at_y[shift[1]], "grp": at_z[shift[2]]}

    y_recv[...] = jnp.zeros_like(y_recv)
    z_recv[...] = jnp.zeros_like(z_recv)
    ny_recv[...] = jnp.zeros_like(ny_recv)
    nc_recv[...] = jnp.zeros_like(nc_recv)
    nz_recv[...] = jnp.zeros_like(nz_recv)
    barrier = pltpu.get_barrier_semaphore()

    def greet(group):
        for shift in members(group):
            pl.semaphore_signal(barrier, inc=1, device_id=device(shift), device_id_type=MESH)

    for group, test in groups.items():
        guarded(test, lambda group=group: greet(group))

    rock = rock_ref[...]

    def rock_row(row):
        value = jnp.full(rock.shape, table_ref[row, 0], jnp.float32)
        for kind in range(1, table_ref.shape[1]):
            value = jnp.where(rock == kind, table_ref[row, kind], value)
        return value

    sat = sat_ref[...]
    cond[...] = perm_ref[...] * (
        jnp.exp(rock_row(0) * jnp.log(sat)) + 2.0 * jnp.exp(rock_row(1) * jnp.log(1.0 - sat))
    )
    p[...] = p0_ref[...]

    def span(axis):
        return 1 + has[axis, 0].astype(jnp.int32) + has[axis, 1].astype(jnp.int32)

    wide = 2 if count_x == 2 else 3
    pl.semaphore_wait(barrier, span("gy") * (3 + wide * (span("grp") - 1)) - 1)

    lane2 = lax.broadcasted_iota(jnp.int32, (cy, cz), 1)

    def exchange(copies):
        for axis, side, copy in copies:
            when((axis, side), copy.start)
        return copies

    def finish(copies):
        for axis, side, copy in copies:
            when((axis, side), copy.wait_send)
            when((axis, 1 - side), copy.wait_recv)

    def remote(axis, side, src, dst, send_sem, recv_sem):
        return (
            axis,
            side,
            pltpu.make_async_remote_copy(
                src_ref=src,
                dst_ref=dst,
                send_sem=send_sem,
                recv_sem=recv_sem,
                device_id={axis: peer[(axis, side)]},
                device_id_type=MESH,
            ),
        )

    def face_start(field, slot):
        for i in range(cx):
            y_send[slot, 0, i : i + 1, :] = field[i, 0:1, :]
            y_send[slot, 1, i : i + 1, :] = field[i, cy - 1 : cy, :]
        packed = jnp.zeros((cy, cz), jnp.float32)
        for i in range(cx):
            plane = field[i]
            packed = jnp.where(lane2 == i, pltpu.roll(plane, i, 1) if i else plane, packed)
            packed = jnp.where(lane2 == cx + i, pltpu.roll(plane, cx + i + 1, 1), packed)
        z_send[slot] = packed
        copies = []
        for side in (0, 1):
            at = 1 - side
            copies.append(
                remote(
                    "grp", side, z_send.at[slot], z_recv.at[slot, at],
                    fs_sem.at[slot, side], fr_sem.at[slot, at],
                )
            )
            copies.append(
                remote(
                    "gy", side, y_send.at[slot, side], y_recv.at[slot, at],
                    fs_sem.at[slot, 2 + side], fr_sem.at[slot, 2 + at],
                )
            )
            copies.append(
                remote(
                    "gx", side, field.at[side * (cx - 1)], x_recv.at[slot, at],
                    fs_sem.at[slot, 4 + side], fr_sem.at[slot, 4 + at],
                )
            )
        return exchange(copies)

    lane3 = lax.broadcasted_iota(jnp.int32, (cx, cy, cz), 2)
    sub3 = lax.broadcasted_iota(jnp.int32, (cx, cy, cz), 1)

    def views(field, slot):
        value = field[...]
        z_left = z_recv[slot, 0]
        z_right = z_recv[slot, 1]
        from_left = jnp.stack([pltpu.roll(z_left, cz - cx - i, 1) for i in range(cx)])
        from_right = jnp.stack([pltpu.roll(z_right, cz - 1 - i, 1) for i in range(cx)])
        y_left = jnp.stack(
            [jnp.broadcast_to(y_recv[slot, 0, i : i + 1, :], (cy, cz)) for i in range(cx)]
        )
        y_right = jnp.stack(
            [jnp.broadcast_to(y_recv[slot, 1, i : i + 1, :], (cy, cz)) for i in range(cx)]
        )
        return (
            jnp.concatenate([x_recv[slot, 0][None], value[:-1]], axis=0),
            jnp.concatenate([value[1:], x_recv[slot, 1][None]], axis=0),
            jnp.where(sub3 == 0, y_left, pltpu.roll(value, 1, 1)),
            jnp.where(sub3 == cy - 1, y_right, pltpu.roll(value, cy - 1, 1)),
            jnp.where(lane3 == 0, from_left, pltpu.roll(value, 1, 2)),
            jnp.where(lane3 == cz - 1, from_right, pltpu.roll(value, cz - 1, 2)),
        )

    cond_copies = face_start(cond, 0)
    first_copies = face_start(p, 1)

    storage = rock_row(2)
    stress[...] = rock_row(3)
    biot[...] = rock_row(4)
    plane_size = cy * count_y * cz * count_z
    flat = (
        (lax.broadcasted_iota(jnp.int32, (cx, cy, cz), 0) + gx * cx) * plane_size
        + (sub3 + gy * cy) * (cz * count_z)
        + lane3
        + gz * cz
    )

    def add_well(well, source):
        return source + jnp.where(flat == cells_ref[well], rates_ref[well], 0.0)

    source = lax.fori_loop(
        0, cells_ref.shape[0], add_well, jnp.zeros((cx, cy, cz), jnp.float32)
    )
    base[...] = storage * p0_ref[...] + source

    row = lax.broadcasted_iota(jnp.int32, (8, cz), 0)
    lane = lax.broadcasted_iota(jnp.int32, (8, cz), 1)
    comp = lax.rem(row, 4)
    along_z = row >= 4
    signs = {}
    for dx in (0, 1):
        for dy in (0, 1):
            signs[dx, dy] = jnp.where(
                comp == 0,
                0.25 * (2 * dx - 1),
                jnp.where(
                    comp == 1,
                    0.25 * (2 * dy - 1),
                    jnp.where(comp == 2, jnp.where(along_z, 0.25, -0.25), 0.0),
                ),
            )

    edge = lane == jnp.where(along_z, cz - 1, 0)
    across = lax.rem(lane, cy + 1)
    line_x = {
        -1: lane <= cy,
        0: None,
        1: (lane >= cx * (cy + 1)) & (lane < (cx + 1) * (cy + 1)),
    }
    line_y = {-1: across == 0, 0: None, 1: across == cy}

    def message(slot, shift):
        sx, sy, sz = shift
        code = 9 * (sz + 1) + 3 * (sy + 1) + sx + 1
        if sz:
            src = nz_send.at[slot]
            dst = nz_recv.at[slot, z_place(-sx, -sy, -sz)]
        elif sx and sy:
            src = res.at[(sx + 1) // 2 * cx, (sy + 1) // 2 * cy]
            dst = nc_recv.at[slot, (1 - sx) + (1 - sy) // 2]
        elif sx:
            src = res.at[(sx + 1) // 2 * cx]
            dst = nx_recv.at[slot, (1 - sx) // 2]
        else:
            src = res.at[:, (sy + 1) // 2 * cy]
            dst = ny_recv.at[slot, (1 - sy) // 2]
        return pltpu.make_async_remote_copy(
            src_ref=src,
            dst_ref=dst,
            send_sem=ns_sem.at[slot, code],
            recv_sem=nr_sem.at[slot, 26 - code],
            device_id=device(shift),
            device_id_type=MESH,
        )

    def share_start(slot):
        first = jnp.zeros((8, cz), jnp.float32)
        second = jnp.zeros((8, cz), jnp.float32)
        for x in range(cx + 1):
            for y in range(cy + 1):
                n = x * (cy + 1) + y
                line = res[x, y]
                first = jnp.where(lane == n, pltpu.roll(line, n, 1) if n else line, first)
                second = jnp.where(lane == n, pltpu.roll(line, n + 1, 1), second)
                swapped = pltpu.roll(line, 4, 0)
                moved = jnp.where(along_z, pltpu.roll(swapped, cz - 1, 1), pltpu.roll(swapped, 1, 1))
                res[x, y] = line + jnp.where(edge, 0.0, moved)
        nz_send[slot] = jnp.where(along_z, second, first)

        def go(group):
            for shift in members(group):
                message(slot, shift).start()

        for group, test in groups.items():
            guarded(test, lambda group=group: go(group))

    def share_arrive(slot):
        def arrive(group):
            for shift in members((-group[0], -group[1])):
                message(slot, shift).wait_recv()

        for group, test in groups.items():
            guarded(test, lambda group=group: arrive(group))
        sides = []
        for sz in (-1, 1):
            total = jnp.zeros((8, cz), jnp.float32)
            for sx in (-1, 0, 1):
                for sy in (-1, 0, 1):
                    part = nz_recv[slot, z_place(abs(sx) if count_x == 2 else sx, sy, sz)]
                    turn = (sx * cx * (cy + 1) + sy * cy) % cz
                    part = pltpu.roll(part, turn, 1) if turn else part
                    for test in (line_x[sx], line_y[sy]):
                        if test is not None:
                            part = jnp.where(test, part, 0.0)
                    total = total + part
            sides.append(total)
        return pltpu.roll(jnp.where(along_z, sides[0], sides[1]), 4, 0)

    def z_place(sx, sy, sz):
        return 9 * (sz + 1) // 2 + 3 * (sy + 1) + sx + 1

    def share_line(slot, beside, x, y):
        n = x * (cy + 1) + y
        total = res[x, y] + jnp.where(edge, jnp.broadcast_to(beside[:, n : n + 1], (8, cz)), 0.0)
        if x in (0, cx):
            total = total + nx_recv[slot, x // cx, y]
        if y in (0, cy):
            total = total + ny_recv[slot, y // cy, x]
        if x in (0, cx) and y in (0, cy):
            total = total + nc_recv[slot, 2 * (x // cx) + y // cy]
        return total

    def share_end(slot):
        def sent(group):
            for shift in members(group):
                message(slot, shift).wait_send()

        for group, test in groups.items():
            guarded(test, lambda group=group: sent(group))

    rows = cy * 8
    offset = lax.broadcasted_iota(jnp.int32, (rows, big_ref.shape[2]), 1) - (
        lax.broadcasted_iota(jnp.int32, (rows, big_ref.shape[2]), 0)
    )
    for i in range(cx):
        for q in range(4):
            block = big_ref[i, q * rows : (q + 1) * rows, :].astype(jnp.float32)
            on = offset == (q // 2) * (cy + 1) * 8 + (q % 2) * 8
            entry = jnp.sum(jnp.where(on, block, 0.0), axis=1, keepdims=True)
            diag_ref[i, q] = jnp.broadcast_to(entry, (rows, cz)).reshape(cy, 8, cz)
    for x in range(cx + 1):
        for y in range(cy + 1):
            total = jnp.zeros((8, cz), jnp.float32)
            for dx in (0, 1):
                for dy in (0, 1):
                    i, k = x - dx, y - dy
                    if 0 <= i < cx and 0 <= k < cy:
                        held = jnp.broadcast_to(
                            anch_ref[i, k : k + 1, :].astype(jnp.float32), (8, cz)
                        )
                        total = total + jnp.where(comp == 3, held, diag_ref[i, 2 * dx + dy, k])
            res[x, y] = total
    share_start(0)
    disp[...] = jnp.zeros_like(disp)
    strain[...] = jnp.zeros_like(strain)

    finish(cond_copies)
    centre = cond[...]
    total_den = storage + stress[...]
    for at, other in enumerate(views(cond, 0)):
        link = 2.0 * centre * other / (centre + other)
        trans[at] = link
        total_den = total_den + link
    inv_den[...] = 1.0 / total_den

    def relax(slot):
        total = numer[...]
        for at, other in enumerate(views(p, slot)):
            total = total + trans[at] * other
        p[...] = total * inv_den[...]

    def settle(slot):
        share_start(slot)
        beside = share_arrive(slot)
        for x in range(cx + 1):
            for y in range(cy + 1):
                total = share_line(slot, beside, x, y)
                disp[x, y] = free[x, y] * disp[x, y] + gain[x, y] * total
        share_end(slot)

    for step in range(ITERS):
        numer[...] = base[...] + stress[...] * p[...] - biot[...] * strain[...]

        def flow(turn, carry):
            slot = 1 + step * FLOW_PASSES + turn
            finish(face_start(p, slot))
            relax(slot)
            return carry

        if step == 0:
            finish(first_copies)
            relax(1)
        lax.fori_loop(1 if step == 0 else 0, FLOW_PASSES, flow, 0)
        if step == 0:
            beside = share_arrive(0)
            for x in range(cx + 1):
                for y in range(cy + 1):
                    line = share_line(0, beside, x, y)
                    count = jnp.where(along_z, line[7:8, :], line[3:4, :])
                    keep = jnp.where((count > 0) | (comp == 3), 0.0, 1.0)
                    free[x, y] = keep
                    gain[x, y] = keep * OMEGA / jnp.where(comp == 3, 1.0, line)
            share_end(0)
        bload[...] = biot[...] * p[...]
        for x in range(cx + 1):
            for y in range(cy + 1):
                total = jnp.zeros((8, cz), jnp.float32)
                for dx in (0, 1):
                    for dy in (0, 1):
                        i, k = x - dx, y - dy
                        if 0 <= i < cx and 0 <= k < cy:
                            total = total + signs[dx, dy] * jnp.broadcast_to(
                                bload[i, k : k + 1, :], (8, cz)
                            )
                load[x, y] = total

        def mech(turn, carry):
            slot = 1 + step * MECH_PASSES + turn
            res[...] = load[...]
            for i in range(cx):
                pair = disp[i : i + 2].reshape(2 * (cy + 1) * 8, cz).astype(jnp.bfloat16)
                force = jnp.dot(big_ref[i], pair, preferred_element_type=jnp.float32)
                force = force.reshape(4, cy, 8, cz)
                res[i, 0:cy] = res[i, 0:cy] - force[0]
                res[i, 1 : cy + 1] = res[i, 1 : cy + 1] - force[1]
                res[i + 1, 0:cy] = res[i + 1, 0:cy] - force[2]
                res[i + 1, 1 : cy + 1] = res[i + 1, 1 : cy + 1] - force[3]
            settle(slot)
            return carry

        if step == 0:
            res[...] = load[...]
            settle(1)
        lax.fori_loop(1 if step == 0 else 0, MECH_PASSES, mech, 0)
        for i in range(cx):
            for k in range(cy):
                total = jnp.zeros((8, cz), jnp.float32)
                for dx in (0, 1):
                    for dy in (0, 1):
                        total = total + signs[dx, dy] * disp[i + dx, k + dy]
                strain[i, k : k + 1, :] = jnp.sum(total, axis=0, keepdims=True)

    p_out[...] = p[...]
    s_out[...] = strain[...]


def hand_on(p_ref, s_ref, p_out, s_out):
    p_out[...] = p_ref[...]
    s_out[...] = s_ref[...]


def per_device(
    pressure_start,
    saturation,
    permeability,
    rock_type,
    rock_table,
    well_cells,
    well_rates,
    owner_map,
    stiffness,
    anchored,
):
    cx, cy, cz = pressure_start.shape
    axes = (lax.axis_size("gx"), lax.axis_size("gy"), lax.axis_size("grp"))
    brick_k = brick_blocks(owner_map, stiffness, axes[0], cx * cy)
    rows, cols = corner_maps(cy)
    rows_b, cols_b = jnp.asarray(rows, jnp.bfloat16), jnp.asarray(cols, jnp.bfloat16)
    shaped = brick_k.reshape(cx, cy, 24, 24)
    spread = jnp.einsum(
        "ikrs,ksc->ikrc", shaped, cols_b, preferred_element_type=jnp.float32
    ).astype(jnp.bfloat16)
    big = jnp.einsum(
        "qmr,ikrc->iqkmc", rows_b, spread, preferred_element_type=jnp.float32
    ).astype(jnp.bfloat16)
    big = big.reshape(cx, 4 * cy * 8, cols.shape[2])

    cell = (cx, cy, cz)
    line = (cx + 1, cy + 1, 8, cz)
    flows = 1 + ITERS * FLOW_PASSES
    shares = 1 + ITERS * MECH_PASSES
    f32 = jnp.float32
    vmem = pl.BlockSpec(memory_space=pltpu.VMEM)
    smem = pl.BlockSpec(memory_space=pltpu.SMEM)
    held = pl.pallas_call(
        functools.partial(kernel, axes),
        out_shape=(jax.ShapeDtypeStruct(cell, f32), jax.ShapeDtypeStruct(cell, f32)),
        in_specs=[smem] * 3 + [vmem] * 6,
        out_specs=(vmem, vmem),
        scratch_shapes=[pltpu.VMEM((cx, 4, cy, 8, cz), f32)]
        + [pltpu.VMEM(cell, f32)] * 7
        + [pltpu.VMEM((6,) + cell, f32)]
        + [pltpu.VMEM(cell, f32)] * 2
        + [pltpu.VMEM(line, f32)] * 5
        + [
            pltpu.VMEM((flows, 2, cx, cz), f32),
            pltpu.VMEM((flows, cy, cz), f32),
            pltpu.VMEM((flows, 2, cy, cz), f32),
            pltpu.VMEM((flows, 2, cx, cz), f32),
            pltpu.VMEM((flows, 2, cy, cz), f32),
            pltpu.VMEM((shares, 8, cz), f32),
            pltpu.VMEM((shares, 2, cy + 1, 8, cz), f32),
            pltpu.VMEM((shares, 2, cx + 1, 8, cz), f32),
            pltpu.VMEM((shares, 4, 8, cz), f32),
            pltpu.VMEM((shares, 18, 8, cz), f32),
            pltpu.SemaphoreType.DMA((flows, 6)),
            pltpu.SemaphoreType.DMA((flows, 6)),
            pltpu.SemaphoreType.DMA((shares, 27)),
            pltpu.SemaphoreType.DMA((shares, 27)),
        ],
        compiler_params=pltpu.CompilerParams(collective_id=0, has_side_effects=True),
    )(
        rock_table,
        well_cells,
        well_rates,
        pressure_start,
        saturation,
        permeability,
        rock_type,
        anchored,
        big,
    )
    return pl.pallas_call(
        hand_on,
        out_shape=(jax.ShapeDtypeStruct(cell, f32), jax.ShapeDtypeStruct(cell, f32)),
        in_specs=[vmem] * 2,
        out_specs=(vmem, vmem),
    )(*held)


def solution(mesh):
    cells = P("gx", "gy", "grp")
    placed = (
        cells,
        cells,
        cells,
        cells,
        P(),
        P(),
        P(),
        P("gx", "gy", "grp", None, None),
        P("gx", "gy", "grp", None, None, None, None),
        cells,
    )
    return jax.shard_map(
        per_device, mesh=mesh, in_specs=placed, out_specs=(cells, cells), check_vma=False
    )
```
